256 devices in a mesh: section: 32 (over y, z_lo, core), dp: 8 (over z_hi, x).
Axes of the slice: x: 4, y: 4, z: 8 (z_hi: 2, z_lo: 4; z = z_hi * 4 + z_lo), core: 2. Of those that a mesh axis runs over, the one named last changes fastest.
Arguments:
- activations: bfloat16 [2, 32, 8, 8, 32, 416], P(None, 'section', 'dp'), may hold values from -6 to 6
- stored_inputs: bfloat16 [2, 3, 32, 8, 8, 32, 416], P(None, None, 'section', 'dp'), may hold values from -6 to 6
- cotangents: bfloat16 [2, 32, 8, 8, 32, 416], P(None, 'section', 'dp'), may hold values from -6 to 6
- new_inputs: bfloat16 [2, 2, 8, 8, 32, 416], P(None, None, 'dp'), may hold values from -6 to 6
- loss_grad: bfloat16 [2, 2, 8, 8, 32, 416], P(None, None, 'dp'), may hold values from -6 to 6
- depth_kernel: bfloat16 [32, 2, 1, 5, 5, 416], P('section'), may hold values from -1.25 to 1.25
- depth_bias: float32 [32, 2, 1, 416], P('section'), may hold values from -3 to 3
- mixing: bfloat16 [32, 2, 1, 416, 416], P('section'), may hold values from -0.3125 to 0.3125
Outputs:
- section_outputs: bfloat16 [2, 32, 8, 8, 32, 416], P(None, 'section', 'dp')
- input_grads: bfloat16 [2, 32, 8, 8, 32, 416], P(None, 'section', 'dp')
- grad_kernel: float32 [32, 1, 5, 5, 416], P('section', None, None, None, 'dp')
- grad_bias: float32 [32, 1, 416], P('section', None, 'dp')
- grad_mixing: float32 [32, 1, 416, 416], P('section', None, 'dp')
The draws below stay inside these ranges and needn't reach their ends.
All inputs are finite; a program needn't handle non-finite values.
Results may differ from the reference program's by a relative error of at most 0.0062.
Values may be sent and summed in bfloat16 or wider, within the bound.
No kernel may reach another device: no remote copies, remote signals or barrier semaphores. Data moves between devices by JAX's collectives and lax.ppermute only.
A program may use at most 128 MiB of HBM per device.

```python
import jax
import jax.numpy as jnp
from jax import lax

C = 416
H = 8
W = 32
KS = 5
LAYERS = 1
TICKS = 3
SECTIONS = 32
IMGS = 8


def shard_levels(stream_key, shape, cuts, smallest, largest):
    gain, own = 1.0, jax.random.fold_in(stream_key, 6)
    for dim, shards_of in cuts:
        steps = jnp.exp(jax.random.uniform(jax.random.fold_in(own, dim), (shards_of,), jnp.float32, smallest / len(cuts), largest / len(cuts)))
        gain = gain * jnp.repeat(steps, shape[dim] // shards_of).reshape([-1 if axis == dim else 1 for axis in range(len(shape))])
    return gain


def gaussian(stream_key, shape, scale, most, pieces=(), held_as=jnp.bfloat16):
    values = scale * jax.random.normal(stream_key, shape, jnp.float32)
    if pieces:
        values = values * shard_levels(stream_key, shape, pieces, -0.22, 0.18)
    return jnp.clip(values, -most, most).astype(held_as)


def setup_inputs(seed: int = 0) -> dict:
    key_list = jax.random.split(jax.random.key(seed), 9)
    return {
        "activations": gaussian(key_list[0], (2, SECTIONS, IMGS, H, W, C), 1.0, 6.0, ((1, 32), (2, 8))),
        "stored_inputs": gaussian(key_list[1], (2, TICKS, SECTIONS, IMGS, H, W, C), 1.0, 6.0, ((2, 32), (3, 8))),
        "cotangents": gaussian(key_list[2], (2, SECTIONS, IMGS, H, W, C), 1.0, 6.0, ((1, 32), (2, 8))),
        "new_inputs": gaussian(key_list[3], (2, TICKS - 1, IMGS, H, W, C), 1.0, 6.0, ((2, 8),)),
        "loss_grad": gaussian(key_list[4], (2, TICKS - 1, IMGS, H, W, C), 1.0, 6.0, ((2, 8),)),
        "depth_kernel": gaussian(key_list[5], (SECTIONS, 2, LAYERS, KS, KS, C), (KS * KS) ** -0.5, 1.25, ((0, 32),)),
        "depth_bias": gaussian(key_list[6], (SECTIONS, 2, LAYERS, C), 0.5, 3.0, ((0, 32),), jnp.float32),
        "mixing": gaussian(key_list[7], (SECTIONS, 2, LAYERS, C, C), C ** -0.5, 0.3125, ((0, 32),)),
    }


def depthwise(maps_in, kernel):
    side = kernel.shape[0]
    margin = side // 2
    height = maps_in.shape[1]
    width = maps_in.shape[2]
    padded = jnp.pad(maps_in, ((0, 0), (margin, margin), (margin, margin), (0, 0)))
    running = jnp.zeros(maps_in.shape, maps_in.dtype)
    for tap_row in range(side):
        for tap_col in range(side):
            running = running + padded[:, tap_row:tap_row + height, tap_col:tap_col + width, :] * kernel[tap_row, tap_col]
    return running

def kernel_grad(maps_in, grad_pre, side):
    margin = side // 2
    height = maps_in.shape[1]
    width = maps_in.shape[2]
    padded = jnp.pad(maps_in, ((0, 0), (margin, margin), (margin, margin), (0, 0)))
    tap_list = []
    for tap_row in range(side):
        for tap_col in range(side):
            window = padded[:, tap_row:tap_row + height, tap_col:tap_col + width, :]
            tap_list.append(lax.optimization_barrier(jnp.sum(window * grad_pre, axis=(0, 1, 2))))
    return jnp.stack(tap_list).reshape(side, side, -1)

def layer_forward(maps_in, kernel, bias, mixing):
    channels = maps_in.shape[-1]
    pre_act = depthwise(maps_in.astype(jnp.float32), kernel.astype(jnp.float32)) + bias
    hidden = jax.nn.gelu(pre_act).astype(jnp.bfloat16)
    mixed_out = jnp.dot(hidden.reshape(-1, channels), mixing, preferred_element_type=jnp.float32)
    result = (maps_in.astype(jnp.float32) + mixed_out.reshape(maps_in.shape)).astype(jnp.bfloat16)
    return (pre_act, hidden, result)

def section_forward(maps_in, kernels, biases, mixings):
    for depth_pos in range(kernels.shape[0]):
        maps_in = layer_forward(maps_in, kernels[depth_pos], biases[depth_pos], mixings[depth_pos])[2]
    return maps_in

def section_backward(maps_in, incoming, kernels, biases, mixings):
    channels = maps_in.shape[-1]
    side = kernels.shape[1]
    stored = []
    for depth_pos in range(kernels.shape[0]):
        pre_act, hidden, result = layer_forward(maps_in, kernels[depth_pos], biases[depth_pos], mixings[depth_pos])
        stored.append((maps_in, pre_act, hidden))
        maps_in = result
    kernel_list = []
    bias_list = []
    mixing_list = []
    for depth_pos in reversed(range(kernels.shape[0])):
        layer_in, pre_act, hidden = stored[depth_pos]
        flat_cot = incoming.reshape(-1, channels)
        grad_mix = lax.dot_general(hidden.reshape(-1, channels), flat_cot, (((0,), (0,)), ((), ())), preferred_element_type=jnp.float32)
        back_hidden = lax.dot_general(flat_cot, mixings[depth_pos], (((1,), (1,)), ((), ())), preferred_element_type=jnp.float32).reshape(pre_act.shape)
        grad_pre = jax.vjp(jax.nn.gelu, pre_act)[1](back_hidden)[0]
        bias_list.insert(0, lax.optimization_barrier(jnp.sum(grad_pre, axis=(0, 1, 2))))
        kernel_list.insert(0, kernel_grad(layer_in.astype(jnp.float32), grad_pre, side))
        mixing_list.insert(0, grad_mix)
        flipped = kernels[depth_pos][::-1, ::-1].astype(jnp.float32)
        incoming = (incoming.astype(jnp.float32) + depthwise(grad_pre, flipped)).astype(jnp.bfloat16)
    return (incoming, jnp.stack(kernel_list), jnp.stack(bias_list), jnp.stack(mixing_list))

def reference(activations, stored_inputs, cotangents, new_inputs, loss_grad, depth_kernel, depth_bias, mixing):
    tick_count = stored_inputs.shape[1]
    outputs_all = []
    grads_all = []
    totals_all = []
    for replica in range(2):
        weights = (depth_kernel[:, replica], depth_bias[:, replica], mixing[:, replica])
        current = activations[replica]
        results = current
        for tick_num in range(tick_count):
            results = lax.map(lambda members: section_forward(*members), (current,) + weights)
            if tick_num < tick_count - 1:
                if replica == 0:
                    current = jnp.concatenate([new_inputs[0, tick_num][None], results[:-1]], 0)
                else:
                    current = jnp.concatenate([results[1:], new_inputs[1, tick_num][None]], 0)
        outputs_all.append(results)
        incoming = cotangents[replica]
        totals = None
        backed = None
        for tick_num in range(tick_count):
            backed = lax.map(lambda members: section_backward(*members), (stored_inputs[replica, tick_num], incoming) + weights)
            if totals is None:
                totals = backed[1:]
            else:
                totals = tuple((left + right for left, right in zip(totals, backed[1:])))
            if tick_num < tick_count - 1:
                if replica == 0:
                    incoming = jnp.concatenate([backed[0][1:], loss_grad[0, tick_num][None]], 0)
                else:
                    incoming = jnp.concatenate([loss_grad[1, tick_num][None], backed[0][:-1]], 0)
        grads_all.append(backed[0])
        totals_all.append(totals)
    factor = (2.0 * tick_count * activations.shape[2] * activations.shape[3] * activations.shape[4]) ** (-0.5)
    summed = tuple(((totals_all[0][j] + totals_all[1][j][::-1]) * factor for j in range(3)))
    return (jnp.stack(outputs_all), jnp.stack(grads_all), summed[0], summed[1], summed[2])
```

```python
import functools

import jax
import jax.numpy as jnp
from jax import lax
from jax.experimental import pallas as pl
from jax.experimental.pallas import tpu as pltpu
from jax.sharding import PartitionSpec as P

F32 = jnp.float32
BF16 = jnp.bfloat16
LANES = 128
SUB = 8
SLOPE = 0.7978845608028654
CUBE = 0.044715


def tiles_of(channels):
    return -(-channels // LANES)


def span_of(tile, channels):
    return min(LANES, channels - tile * LANES)


def clear_margins(pad_ref, channels):
    tiles, height, rows, _ = pad_ref.shape
    zero = jnp.zeros((SUB, LANES), F32)
    for tile in range(tiles):
        full = span_of(tile, channels) < LANES
        for row in range(height):
            starts = range(0, rows, SUB) if full else (0, rows - SUB)
            for start in starts:
                pad_ref[tile, row, pl.ds(start, SUB), :] = zero


def fill(pad_ref, row, block, channels):
    width = block.shape[0]
    for tile in range(pad_ref.shape[0]):
        span = span_of(tile, channels)
        pad_ref[tile, row, pl.ds(SUB, width), 0:span] = block[:, tile * LANES : tile * LANES + span]


def load_params(kernel_ref, bias_ref, replica, taps_ref, shift_ref, channels):
    side = kernel_ref.shape[3]
    tiles = taps_ref.shape[0]
    taps_ref[tiles - 1] = jnp.zeros(taps_ref.shape[1:], F32)
    if shift_ref is not None:
        shift_ref[tiles - 1] = jnp.zeros(shift_ref.shape[1:], F32)
    for tap_row in range(side):
        rows = kernel_ref[0, replica, 0, tap_row].astype(F32)
        for tile in range(tiles):
            span = span_of(tile, channels)
            taps_ref[tile, pl.ds(tap_row * side, side), 0:span] = rows[:, tile * LANES : tile * LANES + span]
    if shift_ref is not None:
        rows = bias_ref[0, replica]
        for tile in range(tiles):
            span = span_of(tile, channels)
            shift_ref[tile, 0:1, 0:span] = rows[:, tile * LANES : tile * LANES + span]


def spread(ref, tile, row):
    return jnp.broadcast_to(ref[tile, pl.ds(row, 1), :], (SUB, LANES))


def conv_tile(pad_ref, taps_ref, tile, side, flip, emit):
    margin = side // 2
    height = pad_ref.shape[1]
    width = pad_ref.shape[2] - 2 * SUB
    last = side * side - 1
    taps = [
        [spread(taps_ref, tile, last - (a * side + b) if flip else a * side + b) for b in range(side)]
        for a in range(side)
    ]
    for start in range(0, width, SUB):
        running = {}
        for source in range(height):
            window = [pad_ref[tile, source, pl.ds(SUB + start - margin + b, SUB), :] for b in range(side)]
            for a in range(side):
                row = source - (a - margin)
                if 0 <= row < height:
                    for b in range(side):
                        term = taps[a][b] * window[b]
                        running[row] = running[row] + term if row in running else term
            done = [r for r in sorted(running) if r + margin <= source or source == height - 1]
            for row in done:
                emit(row, start, running.pop(row))


def tap_grads(pad_ref, grad_ref, tile, side, acc_ref):
    margin = side // 2
    height = pad_ref.shape[1]
    width = pad_ref.shape[2] - 2 * SUB
    sums = [None] * (side * side)
    total = None
    for start in range(0, width, SUB):
        held = {}
        for source in range(height):
            window = [pad_ref[tile, source, pl.ds(SUB + start - margin + b, SUB), :] for b in range(side)]
            for a in range(side):
                row = source - (a - margin)
                if 0 <= row < height:
                    if row not in held:
                        held[row] = grad_ref[tile, row, pl.ds(SUB + start, SUB), :]
                        total = held[row] if total is None else total + held[row]
                    for b in range(side):
                        term = held[row] * window[b]
                        at = a * side + b
                        sums[at] = term if sums[at] is None else sums[at] + term
            held.pop(source - margin, None)
    for at, value in enumerate(sums + [total]):
        acc_ref[tile, pl.ds(at, 1), :] = jnp.sum(value, axis=0, keepdims=True)


def gelu_parts(u, slope):
    square = u * u
    t = jnp.tanh(u * (SLOPE + (SLOPE * CUBE) * square))
    half = 0.5 * (1.0 + t)
    hidden = u * half
    if not slope:
        return hidden, None
    rate = half + hidden * (1.0 - t) * (SLOPE + (3.0 * SLOPE * CUBE) * square)
    return hidden, rate


def activate(pad_ref, taps_ref, shift_ref, side, act_ref, rate_ref, rate_at):
    def body(tile, carry):
        shift = spread(shift_ref, tile, 0)

        def emit(row, start, value):
            hidden, rate = gelu_parts(value + shift, rate_ref is not None)
            act_ref[tile, row, pl.ds(start, SUB), :] = hidden
            if rate_ref is not None:
                rate_ref[rate_at + (tile, row, pl.ds(start, SUB))] = rate

        conv_tile(pad_ref, taps_ref, tile, side, False, emit)
        return carry

    lax.fori_loop(0, pad_ref.shape[0], body, 0)


def pack_hidden(act_ref, hid_ref, hid_at, channels):
    tiles, height, width, _ = act_ref.shape
    for tile in range(tiles):
        span = span_of(tile, channels)
        for row in range(height):
            hid_ref[hid_at + (pl.ds(row * width, width), pl.ds(tile * LANES, span))] = act_ref[
                tile, row, :, 0:span
            ].astype(BF16)


def run_forward(read, params, replica, scratch, write, channels, side):
    kernel_ref, bias_ref, mixing_ref = params
    pad_ref, taps_ref, shift_ref, act_ref, hid_ref = scratch
    height, width = act_ref.shape[1:3]
    load_params(kernel_ref, bias_ref, replica, taps_ref, shift_ref, channels)
    for row in range(height):
        fill(pad_ref, row, read(row).astype(F32), channels)
    activate(pad_ref, taps_ref, shift_ref, side, act_ref, None, None)
    pack_hidden(act_ref, hid_ref, (), channels)
    mixed = jnp.dot(hid_ref[...], mixing_ref[0, replica, 0], preferred_element_type=F32)
    for row in range(height):
        write(row, (read(row).astype(F32) + mixed[row * width : (row + 1) * width]).astype(BF16))


def run_recompute(stored_ref, params, replica, scratch, hid_ref, hid_at, rate_ref, rate_at, channels, side):
    kernel_ref, bias_ref, _ = params
    pad_ref, taps_ref, shift_ref, act_ref = scratch
    height = act_ref.shape[1]
    load_params(kernel_ref, bias_ref, replica, taps_ref, shift_ref, channels)
    for row in range(height):
        fill(pad_ref, row, stored_ref[replica, 0, 0, 0, row].astype(F32), channels)
    activate(pad_ref, taps_ref, shift_ref, side, act_ref, rate_ref, rate_at)
    pack_hidden(act_ref, hid_ref, hid_at, channels)


def run_backward(read, params, replica, pads, taps_ref, work, rate_ref, rate_at, write, acc_ref, channels, side):
    _, _, mixing_ref = params
    pad_ref, slope_ref = pads
    back_ref, dx_ref, flat_ref = work
    tiles, height, width, _ = dx_ref.shape
    for row in range(height):
        flat_ref[pl.ds(row * width, width), :] = read(row)
    back_ref[:, 0:channels] = lax.dot_general(
        flat_ref[...], mixing_ref[0, replica, 0], (((1,), (1,)), ((), ())), preferred_element_type=F32
    )
    for tile in range(tiles):
        for row in range(height):
            slope_ref[tile, row, pl.ds(SUB, width), :] = (
                back_ref[pl.ds(row * width, width), pl.ds(tile * LANES, LANES)] * rate_ref[rate_at + (tile, row)]
            )

    def body(tile, carry):
        def emit(row, start, value):
            dx_ref[tile, row, pl.ds(start, SUB), :] = value

        conv_tile(slope_ref, taps_ref, tile, side, True, emit)
        tap_grads(pad_ref, slope_ref, tile, side, acc_ref)
        return carry

    lax.fori_loop(0, tiles, body, 0)
    for row in range(height):
        for tile in range(tiles):
            span = span_of(tile, channels)
            write(
                row,
                tile,
                span,
                (
                    dx_ref[tile, row, :, 0:span]
                    + flat_ref[pl.ds(row * width, width), pl.ds(tile * LANES, span)].astype(F32)
                ).astype(BF16),
            )


def mix_grad(hid_ref, flat_ref):
    return lax.dot_general(hid_ref, flat_ref, (((0,), (0,)), ((), ())), preferred_element_type=F32)


def writer(ref, lead):
    def write(row, tile, span, block):
        ref[lead + (row, slice(None), pl.ds(tile * LANES, span))] = block

    return write


def first_backward(channels, side, stored_ref, cot_ref, kernel_ref, bias_ref, mixing_ref,
                   gxa_ref, gxb_ref, hid_ref, acc_ref,
                   pad_ref, slope_ref, taps_ref, shift_ref, act_ref, rate_ref, back_ref, dx_ref, flat_ref):
    params = (kernel_ref, bias_ref, mixing_ref)
    clear_margins(pad_ref, channels)
    clear_margins(slope_ref, channels)
    back_ref[:, pl.ds((back_ref.shape[1] // LANES - 1) * LANES, LANES)] = jnp.zeros((back_ref.shape[0], LANES), F32)
    for replica, out_ref in ((0, gxa_ref), (1, gxb_ref)):
        run_recompute(stored_ref, params, replica, (pad_ref, taps_ref, shift_ref, act_ref),
                      hid_ref, (replica,), rate_ref, (), channels, side)
        run_backward(lambda row: cot_ref[replica, 0, 0, row], params, replica, (pad_ref, slope_ref), taps_ref,
                     (back_ref, dx_ref, flat_ref), rate_ref, (), writer(out_ref, ()), acc_ref.at[replica], channels, side)


def forward_recompute(channels, side, entering, *refs):
    refs = list(refs)
    if entering:
        recv_a_ref, recv_b_ref, new_ref = refs[:3]
        refs = refs[3:]
        at_start = lax.axis_index("section") == 0
        at_end = lax.axis_index("section") == lax.axis_size("section") - 1

        def reader(replica):
            flag, ref = ((at_start, recv_a_ref), (at_end, recv_b_ref))[replica]
            return lambda row: jnp.where(flag, new_ref[replica, 0, 0, row].astype(F32), ref[row].astype(F32)).astype(BF16)
    else:
        act_in_ref = refs[0]
        refs = refs[1:]

        def reader(replica):
            return lambda row: act_in_ref[replica, 0, 0, row]

    (stored_ref, kernel_ref, bias_ref, mixing_ref, fa_ref, fb_ref, hid_ref, rate_ref,
     pad_ref, taps_ref, shift_ref, act_ref, mid_ref, x_ref) = refs
    params = (kernel_ref, bias_ref, mixing_ref)
    clear_margins(pad_ref, channels)
    for replica, out_ref in ((0, fa_ref), (1, fb_ref)):
        read = reader(replica)
        for row in range(x_ref.shape[0]):
            x_ref[row] = read(row)

        def write(row, block):
            out_ref[row] = block

        run_forward(lambda row: x_ref[row], params, replica, (pad_ref, taps_ref, shift_ref, act_ref, mid_ref), write,
                    channels, side)
        run_recompute(stored_ref, params, replica, (pad_ref, taps_ref, shift_ref, act_ref),
                      hid_ref, (replica,), rate_ref, (replica,), channels, side)


def last_forward(channels, side, recv_a_ref, recv_b_ref, new_ref, kernel_ref, bias_ref, mixing_ref, out_ref,
                 pad_ref, taps_ref, shift_ref, act_ref, mid_ref, x_ref):
    params = (kernel_ref, bias_ref, mixing_ref)
    clear_margins(pad_ref, channels)
    at_start = lax.axis_index("section") == 0
    at_end = lax.axis_index("section") == lax.axis_size("section") - 1
    for replica, flag, ref in ((0, at_start, recv_a_ref), (1, at_end, recv_b_ref)):
        for row in range(x_ref.shape[0]):
            x_ref[row] = jnp.where(flag, new_ref[replica, 0, 0, row].astype(F32), ref[row].astype(F32)).astype(BF16)

        def write(row, block):
            out_ref[replica, 0, 0, row] = block

        run_forward(lambda row: x_ref[row], params, replica, (pad_ref, taps_ref, shift_ref, act_ref, mid_ref), write,
                    channels, side)


def later_backward(channels, side, last, recv_a_ref, recv_b_ref, loss_ref, stored_ref, hid_ref, rate_ref, *refs):
    refs = list(refs)
    if last:
        part_ref, accin_ref, kernel_ref, bias_ref, mixing_ref, grads_ref, send_ref = refs[:7]
        refs = refs[7:]
        outs = (writer(grads_ref, (0, 0, 0)), writer(grads_ref, (1, 0, 0)))
    else:
        hid0_ref, cot_ref, accin_ref, kernel_ref, bias_ref, mixing_ref, gxa_ref, gxb_ref, part_ref, acc_ref = refs[:10]
        refs = refs[10:]
        outs = (writer(gxa_ref, ()), writer(gxb_ref, ()))
    pad_ref, slope_ref, taps_ref, back_ref, dx_ref, flat_ref, local_ref = refs[:7]
    refs = refs[7:]
    params = (kernel_ref, bias_ref, mixing_ref)
    height, width = dx_ref.shape[1:3]
    clear_margins(pad_ref, channels)
    clear_margins(slope_ref, channels)
    back_ref[:, pl.ds((back_ref.shape[1] // LANES - 1) * LANES, LANES)] = jnp.zeros((back_ref.shape[0], LANES), F32)
    at_start = lax.axis_index("section") == 0
    at_end = lax.axis_index("section") == lax.axis_size("section") - 1
    for replica, flag, ref in ((0, at_end, recv_a_ref), (1, at_start, recv_b_ref)):
        load_params(kernel_ref, bias_ref, replica, taps_ref, None, channels)
        for row in range(height):
            fill(pad_ref, row, stored_ref[replica, 0, 0, 0, row].astype(F32), channels)

        def read(row):
            return jnp.where(flag, loss_ref[replica, 0, 0, row].astype(F32), ref[row].astype(F32)).astype(BF16)

        run_backward(read, params, replica, (pad_ref, slope_ref), taps_ref, (back_ref, dx_ref, flat_ref),
                     rate_ref, (replica,), outs[replica], local_ref, channels, side)
        mixed = mix_grad(hid_ref[replica], flat_ref[...])
        if last:
            rows_ref, turn_ref, stage_ref = refs
            pack_grads(channels, side * side + 1, replica, mixed, part_ref, local_ref, accin_ref, rows_ref, turn_ref, stage_ref, send_ref)
        else:
            for row in range(height):
                flat_ref[pl.ds(row * width, width), :] = cot_ref[replica, 0, 0, row]
            part_ref[replica] = mixed + mix_grad(hid0_ref[replica], flat_ref[...])
            acc_ref[replica] = accin_ref[replica] + local_ref[...]


def pack_grads(channels, used, replica, mixed, part_ref, local_ref, accin_ref, rows_ref, turn_ref, stage_ref, send_ref):
    tiles = tiles_of(channels)
    shards, both, _ = send_ref.shape
    share = both // 2
    edge = span_of(tiles - 1, channels)
    total = mixed + part_ref[replica]
    for tile in range(tiles):
        span = span_of(tile, channels)
        rows_ref[tile, :, 0:span] = total[:, tile * LANES : tile * LANES + span]
    for tile in range(tiles):
        span = span_of(tile, channels)
        count = used
        turn_ref[...] = jnp.zeros(turn_ref.shape, F32)
        turn_ref[pl.ds(edge, count), :] = local_ref[tile, 0:count] + accin_ref[replica, tile, 0:count]
        turned = jnp.transpose(turn_ref[...])
        rows_ref[tiles - 1, pl.ds(tile * LANES, span), edge:LANES] = turned[0:span, edge:LANES]
    for shard in range(shards):
        for tile in range(tiles):
            stage_ref[shard, tile, pl.ds(replica * share, share), :] = rows_ref[tile, pl.ds(shard * share, share), :]
    if replica == 1:
        for shard in range(shards):
            for tile in range(tiles):
                send_ref[shard, :, pl.ds(tile * LANES, LANES)] = stage_ref[shard, tile].astype(BF16)


def sum_shares(recv_ref, own_ref, cross_ref):
    shards, both, _ = recv_ref.shape
    share = both // 2
    total = recv_ref[0].astype(F32)
    for shard in range(1, shards):
        total = total + recv_ref[shard].astype(F32)
    own_ref[...] = total[0:share]
    cross_ref[...] = total[share:both].astype(BF16)


def finish(channels, side, factor, own_ref, cross_ref, kernel_ref, bias_ref, mixing_ref, turn_ref):
    share = own_ref.shape[0]
    edge = channels % LANES
    base = (tiles_of(channels) - 1) * LANES
    total = (own_ref[...] + cross_ref[...].astype(F32)) * factor
    mixing_ref[0, 0] = total[:, 0:channels]
    turn_ref[...] = jnp.zeros(turn_ref.shape, F32)
    turn_ref[0:share, :] = total[:, base : base + LANES]
    turned = jnp.transpose(turn_ref[...])
    for tap_row in range(side):
        kernel_ref[0, 0, tap_row] = turned[edge + tap_row * side : edge + (tap_row + 1) * side, 0:share]
    bias_ref[0] = turned[edge + side * side : edge + side * side + 1, 0:share]


def whole(array):
    return pl.BlockSpec(array.shape, lambda step: (0,) * len(array.shape))


def tick_of(array, tick):
    shape = (array.shape[0], 1) + array.shape[2:]
    return pl.BlockSpec(shape, lambda step: (0, tick) + (0,) * (len(shape) - 2))


def call(body, args, outs, scratch, name):
    specs = [whole(a) if not isinstance(a, tuple) else tick_of(*a) for a in args]
    args = [a if not isinstance(a, tuple) else a[0] for a in args]
    return pl.pallas_call(
        body,
        out_shape=outs,
        grid=(1,),
        in_specs=specs,
        out_specs=jax.tree.map(whole, outs),
        scratch_shapes=scratch,
        name=name,
        compiler_params=pltpu.CompilerParams(vmem_limit_bytes=40 * 1024 * 1024),
    )(*args)


def move(block, distance):
    count = lax.axis_size("section")
    route = [(i - distance, i) for i in range(count) if 0 <= i - distance < count]
    return lax.ppermute(block, "section", route)


def per_device(activations, stored_inputs, cotangents, new_inputs, loss_grad, depth_kernel, depth_bias, mixing):
    sections = lax.axis_size("section")
    shards = lax.axis_size("dp")
    height, width, channels = activations.shape[3:]
    side = depth_kernel.shape[3]
    tick_count = stored_inputs.shape[1]
    tiles = tiles_of(channels)
    wide = tiles * LANES
    spots = height * width
    params = (depth_kernel, depth_bias, mixing)
    struct = jax.ShapeDtypeStruct
    maps = struct((height, width, channels), BF16)
    hids = struct((2, spots, channels), BF16)
    rates = struct((2, tiles, height, width, LANES), F32)
    accs = struct((2, tiles, 32, LANES), F32)
    parts = struct((2, channels, channels), F32)
    pad = pltpu.VMEM((tiles, height, width + 2 * SUB, LANES), F32)
    taps = pltpu.VMEM((tiles, 32, LANES), F32)
    shift = pltpu.VMEM((tiles, SUB, LANES), F32)
    act = pltpu.VMEM((tiles, height, width, LANES), F32)
    back = pltpu.VMEM((spots, wide), F32)
    flat = pltpu.VMEM((spots, channels), BF16)
    local = pltpu.VMEM((tiles, 32, LANES), F32)
    bind = functools.partial

    gxa, gxb, hid0, acc = call(
        bind(first_backward, channels, side), ((stored_inputs, 0), cotangents) + params,
        (maps, maps, hids, accs), [pad, pad, taps, shift, act, act, back, act, flat], "back0")
    ga = move(gxa, -1)
    gb = move(gxb, 1)
    fscratch = [pad, taps, shift, act, flat, pltpu.VMEM((height, width, channels), BF16)]
    fa, fb, hid1, rate = call(
        bind(forward_recompute, channels, side, False), (activations, (stored_inputs, 1)) + params,
        (maps, maps, hids, rates), fscratch, "fwd0")
    xa = move(fa, 1)
    xb = move(fb, -1)
    bscratch = [pad, pad, taps, back, act, flat, local]
    gxa, gxb, part, acc = call(
        bind(later_backward, channels, side, False),
        (ga, gb, (loss_grad, 0), (stored_inputs, 1), hid1, rate, hid0, cotangents, acc) + params,
        (maps, maps, parts, accs), bscratch, "back1")
    ga = move(gxa, -1)
    gb = move(gxb, 1)
    fa, fb, hid2, rate = call(
        bind(forward_recompute, channels, side, True), (xa, xb, (new_inputs, 0), (stored_inputs, 2)) + params,
        (maps, maps, hids, rates), fscratch, "fwd1")
    xa = move(fa, 1)
    xb = move(fb, -1)
    share = channels // shards
    both = struct((shards, 2 * share, wide), BF16)
    pair = struct((2, 1, 1, height, width, channels), BF16)
    input_grads, send = call(
        bind(later_backward, channels, side, True),
        (ga, gb, (loss_grad, 1), (stored_inputs, 2), hid2, rate, part, acc) + params,
        (pair, both),
        bscratch + [pltpu.VMEM((tiles, channels, LANES), F32), pltpu.VMEM((LANES, LANES), F32),
                    pltpu.VMEM((shards, tiles, 2 * share, LANES), F32)], "back2")
    spread_out = lax.all_to_all(send, "dp", split_axis=0, concat_axis=0, tiled=True)
    section_outputs = call(
        bind(last_forward, channels, side), (xa, xb, (new_inputs, 1)) + params, pair, fscratch, "fwd2")
    own, cross = call(
        sum_shares, (spread_out,), (struct((share, wide), F32), struct((share, wide), BF16)), [], "shares")
    cross = lax.ppermute(cross, "section", [(i, sections - 1 - i) for i in range(sections)])
    factor = float((2.0 * tick_count * shards * spots) ** (-0.5))
    grad_kernel, grad_bias, grad_mixing = call(
        bind(finish, channels, side, factor), (own, cross),
        (struct((1, 1, side, side, share), F32), struct((1, 1, share), F32), struct((1, 1, share, channels), F32)),
        [pltpu.VMEM((LANES, LANES), F32)], "finish")
    return (section_outputs, input_grads, grad_kernel, grad_bias, grad_mixing)


def solution(mesh):
    return jax.shard_map(
        per_device,
        mesh=mesh,
        in_specs=(
            P(None, "section", "dp", None, None, None),
            P(None, None, "section", "dp", None, None, None),
            P(None, "section", "dp", None, None, None),
            P(None, None, "dp", None, None, None),
            P(None, None, "dp", None, None, None),
            P("section", None, None, None, None, None),
            P("section", None, None, None),
            P("section", None, None, None, None),
        ),
        out_specs=(
            P(None, "section", "dp", None, None, None),
            P(None, "section", "dp", None, None, None),
            P("section", None, None, None, "dp"),
            P("section", None, "dp"),
            P("section", None, "dp", None),
        ),
        check_vma=False,
    )
```

```python
import functools

import jax
import jax.numpy as jnp
from jax import lax
from jax.experimental import pallas as pl
from jax.experimental.pallas import tpu as pltpu
from jax.sharding import PartitionSpec as P

F32 = jnp.float32
BF16 = jnp.bfloat16
LANES = 128
SUB = 8
SLOPE = 0.7978845608028654
CUBE = 0.044715


def tiles_of(channels):
    return -(-channels // LANES)


def span_of(tile, channels):
    return min(LANES, channels - tile * LANES)


def clear_margins(pad_ref, channels):
    tiles, height, rows, _ = pad_ref.shape
    zero = jnp.zeros((SUB, LANES), F32)
    for tile in range(tiles):
        full = span_of(tile, channels) < LANES
        for row in range(height):
            starts = range(0, rows, SUB) if full else (0, rows - SUB)
            for start in starts:
                pad_ref[tile, row, pl.ds(start, SUB), :] = zero


def fill(pad_ref, row, block, channels):
    width = block.shape[0]
    for tile in range(pad_ref.shape[0]):
        span = span_of(tile, channels)
        pad_ref[tile, row, pl.ds(SUB, width), 0:span] = block[:, tile * LANES : tile * LANES + span]


def load_taps(kernel_ref, taps_ref, channels):
    tiles = taps_ref.shape[0]
    for tap in range(kernel_ref.shape[0]):
        rows = kernel_ref[tap].astype(F32)
        for tile in range(tiles):
            span = span_of(tile, channels)
            if span < LANES:
                taps_ref[tile, tap] = jnp.zeros(taps_ref.shape[2:], F32)
            taps_ref[tile, tap, :, 0:span] = rows[:, tile * LANES : tile * LANES + span]


def load_shift(bias_ref, shift_ref, channels):
    for replica in range(2):
        rows = bias_ref[0, replica]
        for tile in range(shift_ref.shape[0]):
            span = span_of(tile, channels)
            if span < LANES:
                shift_ref[tile, replica] = jnp.zeros(shift_ref.shape[2:], F32)
            shift_ref[tile, replica, 0:1, 0:span] = rows[:, tile * LANES : tile * LANES + span]


def conv_tile(pad_ref, taps_ref, replica, tile, side, flip, emit):
    margin = side // 2
    height = pad_ref.shape[1]
    width = pad_ref.shape[2] - 2 * SUB
    last = side * side - 1
    taps = [
        [
            jnp.broadcast_to(
                taps_ref[tile, last - (a * side + b) if flip else a * side + b, replica : replica + 1, :], (SUB, LANES)
            )
            for b in range(side)
        ]
        for a in range(side)
    ]
    for start in range(0, width, SUB):
        running = {}
        for source in range(height):
            window = [pad_ref[tile, source, pl.ds(SUB + start - margin + b, SUB), :] for b in range(side)]
            for a in range(side):
                row = source - (a - margin)
                if 0 <= row < height:
                    for b in range(side):
                        term = taps[a][b] * window[b]
                        running[row] = running[row] + term if row in running else term
            done = [r for r in sorted(running) if r + margin <= source or source == height - 1]
            for row in done:
                emit(row, start, running.pop(row))


def tap_grads(pad_ref, grad_ref, tile, side, acc_ref):
    margin = side // 2
    height = pad_ref.shape[1]
    width = pad_ref.shape[2] - 2 * SUB
    sums = [None] * (side * side)
    total = None
    for start in range(0, width, SUB):
        held = {}
        for source in range(height):
            window = [pad_ref[tile, source, pl.ds(SUB + start - margin + b, SUB), :] for b in range(side)]
            for a in range(side):
                row = source - (a - margin)
                if 0 <= row < height:
                    if row not in held:
                        held[row] = grad_ref[tile, row, pl.ds(SUB + start, SUB), :]
                        total = held[row] if total is None else total + held[row]
                    for b in range(side):
                        term = held[row] * window[b]
                        at = a * side + b
                        sums[at] = term if sums[at] is None else sums[at] + term
            held.pop(source - margin, None)
    for at, value in enumerate(sums + [total]):
        acc_ref[tile, pl.ds(at, 1), :] = jnp.sum(value, axis=0, keepdims=True)


def gelu_parts(u, slope):
    square = u * u
    t = jnp.tanh(u * (SLOPE + (SLOPE * CUBE) * square))
    half = 0.5 * (1.0 + t)
    hidden = u * half
    if not slope:
        return hidden, None
    rate = half + hidden * (1.0 - t) * (SLOPE + (3.0 * SLOPE * CUBE) * square)
    return hidden, rate


def activate(pad_ref, taps_ref, shift_ref, replica, side, act_ref, rate_ref, rate_at):
    def body(tile, carry):
        shift = jnp.broadcast_to(shift_ref[tile, replica, 0:1, :], (SUB, LANES))

        def emit(row, start, value):
            hidden, rate = gelu_parts(value + shift, rate_ref is not None)
            act_ref[tile, row, pl.ds(start, SUB), :] = hidden
            if rate_ref is not None:
                rate_ref[rate_at + (tile, row, pl.ds(start, SUB))] = rate

        conv_tile(pad_ref, taps_ref, replica, tile, side, False, emit)
        return carry

    lax.fori_loop(0, pad_ref.shape[0], body, 0)


def pack_hidden(act_ref, hid_ref, hid_at, channels):
    tiles, height, width, _ = act_ref.shape
    for tile in range(tiles):
        span = span_of(tile, channels)
        for row in range(height):
            hid_ref[hid_at + (pl.ds(row * width, width), pl.ds(tile * LANES, span))] = act_ref[
                tile, row, :, 0:span
            ].astype(BF16)


def run_forward(read, mixing, replica, taps_ref, shift_ref, scratch, write, channels, side):
    pad_ref, act_ref, mid_ref = scratch
    height, width = act_ref.shape[1:3]
    for row in range(height):
        fill(pad_ref, row, read(row).astype(F32), channels)
    activate(pad_ref, taps_ref, shift_ref, replica, side, act_ref, None, None)
    pack_hidden(act_ref, mid_ref, (), channels)
    mixed = jnp.dot(mid_ref[...], mixing, preferred_element_type=F32)
    for row in range(height):
        write(row, (read(row).astype(F32) + mixed[row * width : (row + 1) * width]).astype(BF16))


def run_recompute(read, replica, taps_ref, shift_ref, scratch, hid_ref, hid_at, rate_ref, rate_at, channels, side):
    pad_ref, act_ref = scratch
    for row in range(act_ref.shape[1]):
        fill(pad_ref, row, read(row).astype(F32), channels)
    activate(pad_ref, taps_ref, shift_ref, replica, side, act_ref, rate_ref, rate_at)
    pack_hidden(act_ref, hid_ref, hid_at, channels)


def run_cotangent(flat_ref, mixing, replica, taps_ref, back_ref, rate_ref, rate_at, slope_ref, dx_ref, write, channels, side):
    tiles, height, width, _ = dx_ref.shape
    back_ref[:, 0:channels] = lax.dot_general(
        flat_ref[...], mixing, (((1,), (1,)), ((), ())), preferred_element_type=F32
    )
    for tile in range(tiles):
        for row in range(height):
            slope_ref[tile, row, pl.ds(SUB, width), :] = (
                back_ref[pl.ds(row * width, width), pl.ds(tile * LANES, LANES)] * rate_ref[rate_at + (tile, row)]
            )

    def body(tile, carry):
        def emit(row, start, value):
            dx_ref[tile, row, pl.ds(start, SUB), :] = value

        conv_tile(slope_ref, taps_ref, replica, tile, side, True, emit)
        return carry

    lax.fori_loop(0, tiles, body, 0)
    for row in range(height):
        for tile in range(tiles):
            span = span_of(tile, channels)
            kept = flat_ref[pl.ds(row * width, width), pl.ds(tile * LANES, span)].astype(F32)
            write(row, tile, span, (dx_ref[tile, row, :, 0:span] + kept).astype(BF16))


def run_taps(pad_ref, slope_ref, side, acc_ref):
    def body(tile, carry):
        tap_grads(pad_ref, slope_ref, tile, side, acc_ref)
        return carry

    lax.fori_loop(0, pad_ref.shape[0], body, 0)


def clear_last(back_ref):
    rows, wide = back_ref.shape
    back_ref[:, wide - LANES : wide] = jnp.zeros((rows, LANES), F32)


def mix_grad(hid_ref, flat_ref):
    return lax.dot_general(hid_ref, flat_ref, (((0,), (0,)), ((), ())), preferred_element_type=F32)


def writer(ref, lead):
    def write(row, tile, span, block):
        ref[lead + (row, slice(None), pl.ds(tile * LANES, span))] = block

    return write


def first_kernel(channels, side, stored_hbm, cot_hbm, kernel_hbm, bias_hbm, mixing_hbm,
                 gxa_ref, gxb_ref, hid_ref, slope_ref,
                 stored_ref, cot_ref, kernel_ref, bias_ref, mixing_ref, sems,
                 pad_ref, taps_ref, shift_ref, act_ref, rate_ref, back_ref, dx_ref):
    copies = [pltpu.make_async_copy(kernel_hbm, kernel_ref, sems.at[0]),
              pltpu.make_async_copy(bias_hbm, bias_ref, sems.at[1])]
    for replica in range(2):
        copies.append(pltpu.make_async_copy(stored_hbm.at[replica, 0, 0, 0], stored_ref.at[replica], sems.at[2 + 3 * replica]))
        copies.append(pltpu.make_async_copy(mixing_hbm.at[0, replica, 0], mixing_ref.at[replica], sems.at[3 + 3 * replica]))
        copies.append(pltpu.make_async_copy(cot_hbm.at[replica, 0, 0], cot_ref.at[replica], sems.at[4 + 3 * replica]))
    for copy in copies:
        copy.start()
    height, width = act_ref.shape[1:3]
    clear_margins(pad_ref, channels)
    clear_last(back_ref)
    for replica in range(2):
        clear_margins(slope_ref.at[replica], channels)
    copies[0].wait()
    copies[1].wait()
    load_taps(kernel_ref, taps_ref, channels)
    load_shift(bias_ref, shift_ref, channels)
    for replica, out_ref in ((0, gxa_ref), (1, gxb_ref)):
        for copy in copies[2 + 3 * replica : 5 + 3 * replica]:
            copy.wait()
        run_recompute(lambda row: stored_ref[replica, row], replica, taps_ref, shift_ref, (pad_ref, act_ref),
                      hid_ref, (replica,), rate_ref, (), channels, side)
        flat_ref = cot_ref.at[replica]
        run_cotangent(flat_ref, mixing_ref[replica], replica, taps_ref, back_ref, rate_ref, (), slope_ref.at[replica],
                      dx_ref, writer(out_ref, ()), channels, side)


def entering(flag, new, old):
    return jnp.where(flag, new.astype(F32), old.astype(F32)).astype(BF16)


def ends():
    spot = lax.axis_index("section")
    return spot == 0, spot == lax.axis_size("section") - 1


def middle_kernel(channels, side, forward, *refs):
    refs = list(refs)
    if forward:
        (act_in_ref, stored_ref, next_ref, slope_ref, kernel_ref, bias_ref, mixing_ref,
         fa_ref, fb_ref, hid_ref, rate_ref, acc_ref, pad_ref, taps_ref, shift_ref, act_ref, mid_ref) = refs
    else:
        (stored_ref, next_ref, slope_ref, accin_ref, hid0_ref, cot_ref, hid1_ref, g1_ref, kernel_ref, bias_ref,
         hid_ref, rate_ref, acc_ref, part_ref, pad_ref, taps_ref, shift_ref, act_ref, local_ref) = refs
    clear_margins(pad_ref, channels)
    load_taps(kernel_ref, taps_ref, channels)
    load_shift(bias_ref, shift_ref, channels)
    for replica in range(2):
        if forward:
            out_ref = (fa_ref, fb_ref)[replica]

            def write(row, block):
                out_ref[row] = block

            run_forward(lambda row: act_in_ref[replica, 0, 0, row], mixing_ref[0, replica, 0], replica, taps_ref, shift_ref,
                        (pad_ref, act_ref, mid_ref), write, channels, side)
        run_recompute(lambda row: next_ref[replica, 0, 0, 0, row], replica, taps_ref, shift_ref, (pad_ref, act_ref),
                      hid_ref, (replica,), rate_ref, (replica,), channels, side)
        for row in range(act_ref.shape[1]):
            fill(pad_ref, row, stored_ref[replica, 0, 0, 0, row].astype(F32), channels)
        if forward:
            run_taps(pad_ref, slope_ref.at[replica], side, acc_ref.at[replica])
        else:
            run_taps(pad_ref, slope_ref.at[replica], side, local_ref)
            acc_ref[replica] = accin_ref[replica] + local_ref[...]
            part_ref[replica] = mix_grad(hid0_ref[replica], cot_ref[replica]) + mix_grad(hid1_ref[replica], g1_ref[replica])


def second_kernel(channels, side, recv_a_ref, recv_b_ref, loss_ref, rate_ref, kernel_ref, mixing_ref,
                  gxa_ref, gxb_ref, slope_ref, g1_ref, taps_ref, back_ref, dx_ref):
    height, width = dx_ref.shape[1:3]
    clear_last(back_ref)
    load_taps(kernel_ref, taps_ref, channels)
    at_start, at_end = ends()
    for replica, flag, ref, out_ref in ((0, at_end, recv_a_ref, gxa_ref), (1, at_start, recv_b_ref, gxb_ref)):
        clear_margins(slope_ref.at[replica], channels)
        for row in range(height):
            g1_ref[replica, pl.ds(row * width, width), :] = entering(flag, loss_ref[replica, 0, 0, row], ref[row])
        run_cotangent(g1_ref.at[replica], mixing_ref[0, replica, 0], replica, taps_ref, back_ref, rate_ref, (replica,),
                      slope_ref.at[replica], dx_ref, writer(out_ref, ()), channels, side)


def third_kernel(channels, side, replica, recv_ref, loss_ref, stored_ref, hid_ref, rate_ref, part_ref, accin_ref,
                 kernel_ref, mixing_ref, *refs):
    refs = list(refs)
    other_ref = refs.pop(0) if replica == 0 else None
    grads_ref, own_ref, one_ref, two_ref, three_ref = refs[:5]
    pad_ref, slope_ref, taps_ref, back_ref, dx_ref, flat_ref, local_ref, rows_ref, turn_ref, stage_ref = refs[5:]
    height, width = dx_ref.shape[1:3]
    clear_margins(pad_ref, channels)
    clear_margins(slope_ref, channels)
    clear_last(back_ref)
    load_taps(kernel_ref, taps_ref, channels)
    at_start, at_end = ends()
    flag = at_start if replica else at_end
    for row in range(height):
        flat_ref[pl.ds(row * width, width), :] = entering(flag, loss_ref[replica, 0, 0, row], recv_ref[row])
        fill(pad_ref, row, stored_ref[replica, 0, 0, 0, row].astype(F32), channels)
    if replica == 0:
        grads_ref[1, 0, 0] = other_ref[...]
        write = writer(grads_ref, (0, 0, 0))
    else:
        write = writer(grads_ref, ())
    run_cotangent(flat_ref, mixing_ref[0, replica, 0], replica, taps_ref, back_ref, rate_ref, (replica,), slope_ref, dx_ref,
                  write, channels, side)
    run_taps(pad_ref, slope_ref, side, local_ref)
    total = mix_grad(hid_ref[replica], flat_ref[...]) + part_ref[replica]
    tiles = tiles_of(channels)
    ring = stage_ref.shape[0]
    both = stage_ref.shape[2]
    share = both // 2
    edge = span_of(tiles - 1, channels)
    count = side * side + 1
    for tile in range(tiles):
        span = span_of(tile, channels)
        rows_ref[tile, :, 0:span] = total[:, tile * LANES : tile * LANES + span]
    for tile in range(tiles):
        span = span_of(tile, channels)
        turn_ref[...] = jnp.zeros(turn_ref.shape, F32)
        turn_ref[pl.ds(edge, count), :] = local_ref[tile, 0:count] + accin_ref[replica, tile, 0:count]
        turned = jnp.transpose(turn_ref[...])
        rows_ref[tiles - 1, pl.ds(tile * LANES, span), edge:LANES] = turned[0:span, edge:LANES]
    for spot in range(ring):
        for half in range(2):
            for tile in range(tiles):
                stage_ref[spot, tile, pl.ds(half * share, share), :] = rows_ref[
                    tile, pl.ds((half * ring + spot) * share, share), :
                ]
    me = lax.rem(lax.axis_index("dp"), ring)
    for tile in range(tiles):
        own_ref[:, pl.ds(tile * LANES, LANES)] = stage_ref[me, tile]
    for step, out_ref in ((1, one_ref), (2, two_ref), (3, three_ref)):
        spot = lax.rem(me + step, ring)
        for tile in range(tiles):
            out_ref[:, pl.ds(tile * LANES, LANES)] = stage_ref[spot, tile].astype(BF16)


def forward_kernel(channels, side, last, recv_a_ref, recv_b_ref, new_ref, kernel_ref, bias_ref, mixing_ref, *refs):
    outs = refs[:1] if last else refs[:2]
    pad_ref, taps_ref, shift_ref, act_ref, mid_ref, x_ref = refs[len(outs):]
    clear_margins(pad_ref, channels)
    load_taps(kernel_ref, taps_ref, channels)
    load_shift(bias_ref, shift_ref, channels)
    at_start, at_end = ends()
    for replica, flag, ref in ((0, at_start, recv_a_ref), (1, at_end, recv_b_ref)):
        for row in range(x_ref.shape[0]):
            x_ref[row] = entering(flag, new_ref[replica, 0, 0, row], ref[row])

        def write(row, block):
            if last:
                outs[0][replica, 0, 0, row] = block
            else:
                outs[replica][row] = block

        run_forward(lambda row: x_ref[row], mixing_ref[0, replica, 0], replica, taps_ref, shift_ref,
                    (pad_ref, act_ref, mid_ref), write, channels, side)


def sum_ring(own_ref, one_ref, two_ref, three_ref):
    return own_ref[...] + one_ref[...].astype(F32) + (two_ref[...].astype(F32) + three_ref[...].astype(F32))


def halves(total):
    share = total.shape[0] // 2
    low = lax.axis_index("dp") < lax.axis_size("dp") // 2
    first, second = total[0:share], total[share : 2 * share]
    return jnp.where(low, first, second), jnp.where(low, second, first)


def sum_b(own_ref, one_ref, two_ref, three_ref, near_ref, far_ref):
    near, far = halves(sum_ring(own_ref, one_ref, two_ref, three_ref))
    near_ref[...] = near.astype(BF16)
    far_ref[...] = far.astype(BF16)


def sum_a(own_ref, one_ref, two_ref, three_ref, near_ref, far_ref):
    near, far = halves(sum_ring(own_ref, one_ref, two_ref, three_ref))
    near_ref[...] = near
    far_ref[...] = far.astype(BF16)


def finish(channels, side, factor, own_ref, far_ref, cross_ref, both_ref, kernel_ref, bias_ref, mixing_ref, turn_ref):
    share = own_ref.shape[0]
    edge = channels % LANES
    base = (tiles_of(channels) - 1) * LANES
    total = own_ref[...] + far_ref[...].astype(F32) + (cross_ref[...].astype(F32) + both_ref[...].astype(F32))
    total = total * factor
    mixing_ref[:, 0, :] = total[:, 0:channels]
    turn_ref[...] = jnp.zeros(turn_ref.shape, F32)
    turn_ref[0:share, :] = total[:, base : base + LANES]
    turned = jnp.transpose(turn_ref[...])
    for tap_row in range(side):
        for tap_col in range(side):
            at = edge + tap_row * side + tap_col
            kernel_ref[tap_row, tap_col] = turned[at : at + 1, 0:share]
    bias_ref[0] = turned[edge + side * side : edge + side * side + 1, 0:share]


def whole(array):
    return pl.BlockSpec(array.shape, lambda step: (0,) * len(array.shape))


def tick_of(array, tick):
    shape = (array.shape[0], 1) + array.shape[2:]
    return pl.BlockSpec(shape, lambda step: (0, tick) + (0,) * (len(shape) - 2))


def call(body, args, outs, scratch, name, hbm=False):
    specs = [whole(a) if not isinstance(a, tuple) else tick_of(*a) for a in args]
    if hbm:
        specs = [pl.BlockSpec(memory_space=pltpu.HBM) for _ in args]
    args = [a if not isinstance(a, tuple) else a[0] for a in args]
    with jax.named_scope(name):
        return pl.pallas_call(
            body,
            out_shape=outs,
            grid=(1,),
            in_specs=specs,
            out_specs=jax.tree.map(whole, outs),
            scratch_shapes=scratch,
            name=name,
            compiler_params=pltpu.CompilerParams(vmem_limit_bytes=20 * 1024 * 1024),
        )(*args)


def move(block, distance, name):
    count = lax.axis_size("section")
    with jax.named_scope(name):
        return lax.ppermute(block, "section", [(i, (i + distance) % count) for i in range(count)])


def per_device(activations, stored_inputs, cotangents, new_inputs, loss_grad, depth_kernel, depth_bias, mixing):
    sections = lax.axis_size("section")
    shards = lax.axis_size("dp")
    ring = shards // 2
    height, width, channels = activations.shape[3:]
    side = depth_kernel.shape[3]
    tick_count = stored_inputs.shape[1]
    tiles = tiles_of(channels)
    wide = tiles * LANES
    spots = height * width
    kernels = jnp.transpose(depth_kernel, (0, 2, 3, 4, 1, 5)).reshape(side * side, 2, channels)
    struct = jax.ShapeDtypeStruct
    maps = struct((height, width, channels), BF16)
    hids = struct((2, spots, channels), BF16)
    rates = struct((2, tiles, height, width, LANES), F32)
    accs = struct((2, tiles, 32, LANES), F32)
    parts = struct((2, channels, channels), F32)
    slopes = struct((2, tiles, height, width + 2 * SUB, LANES), F32)
    pad = pltpu.VMEM((tiles, height, width + 2 * SUB, LANES), F32)
    taps = pltpu.VMEM((tiles, side * side, 2, LANES), F32)
    shift = pltpu.VMEM((tiles, 2, SUB, LANES), F32)
    act = pltpu.VMEM((tiles, height, width, LANES), F32)
    back = pltpu.VMEM((spots, wide), F32)
    flat = pltpu.VMEM((spots, channels), BF16)
    local = pltpu.VMEM((tiles, 32, LANES), F32)
    bind = functools.partial

    flat_cot = cotangents.reshape(2, 1, 1, spots, channels)
    gxa, gxb, hid0, slope = call(
        bind(first_kernel, channels, side), (stored_inputs, flat_cot, kernels, depth_bias, mixing),
        (maps, maps, hids, slopes),
        [pltpu.VMEM((2, height, width, channels), BF16), pltpu.VMEM((2, spots, channels), BF16),
         pltpu.VMEM(kernels.shape, BF16), pltpu.VMEM(depth_bias.shape, F32), pltpu.VMEM((2, channels, channels), BF16),
         pltpu.SemaphoreType.DMA((8,)), pad, taps, shift, act, act, back, act], "back0", hbm=True)
    ga = move(gxa, -1, "pc0a")
    gb = move(gxb, 1, "pc0b")
    fa, fb, hid1, rate, acc = call(
        bind(middle_kernel, channels, side, True),
        (activations, (stored_inputs, 0), (stored_inputs, 1), slope, kernels, depth_bias, mixing),
        (maps, maps, hids, rates, accs), [pad, taps, shift, act, flat], "mid0")
    xa = move(fa, 1, "pf0a")
    xb = move(fb, -1, "pf0b")
    gxa, gxb, slope, g1 = call(
        bind(second_kernel, channels, side), (ga, gb, (loss_grad, 0), rate, kernels, mixing),
        (maps, maps, slopes, hids), [taps, back, act], "back1")
    ga = move(gxa, -1, "pc1a")
    gb = move(gxb, 1, "pc1b")
    hid2, rate, acc, part = call(
        bind(middle_kernel, channels, side, False),
        ((stored_inputs, 1), (stored_inputs, 2), slope, acc, hid0, flat_cot.reshape(2, spots, channels), hid1, g1, kernels, depth_bias),
        (hids, rates, accs, parts), [pad, taps, shift, act, local], "mid1")
    share = channels // shards
    block = struct((2 * share, wide), BF16)
    held = struct((2 * share, wide), F32)
    pair = struct((2, 1, 1, height, width, channels), BF16)
    bscratch = [pad, pad, taps, back, act, flat, local,
                pltpu.VMEM((tiles, channels, LANES), F32), pltpu.VMEM((LANES, LANES), F32),
                pltpu.VMEM((ring, tiles, 2 * share, LANES), F32)]
    common = ((loss_grad, 1), (stored_inputs, 2), hid2, rate, part, acc, kernels, mixing)

    def around(blocks, name):
        got = []
        for step, item in enumerate(blocks, 1):
            route = [(i, i - i % ring + (i + step) % ring) for i in range(shards)]
            with jax.named_scope(name + str(step)):
                got.append(lax.ppermute(item, "dp", route))
        return got

    grads_b, own_b, *send_b = call(
        bind(third_kernel, channels, side, 1), (gb,) + common, (maps, held, block, block, block), bscratch, "back2b")
    got_b = around(send_b, "xb")
    input_grads, own_a, *send_a = call(
        bind(third_kernel, channels, side, 0), (ga,) + common + (grads_b,), (pair, held, block, block, block), bscratch, "back2a")
    got_a = around(send_a, "xa")
    fscratch = [pad, taps, shift, act, flat, pltpu.VMEM((height, width, channels), BF16)]
    fa, fb = call(
        bind(forward_kernel, channels, side, False), (xa, xb, (new_inputs, 0), kernels, depth_bias, mixing),
        (maps, maps), fscratch, "fwd1")
    xa = move(fa, 1, "pf1a")
    xb = move(fb, -1, "pf1b")
    quarter = struct((share, wide), BF16)
    near_b, far_b = call(sum_b, (own_b, *got_b), (quarter, quarter), [], "sumb")
    devices = [(s, d) for s in range(sections) for d in range(shards)]
    with jax.named_scope("mirror"):
        cross = lax.ppermute(near_b, "section", [(i, sections - 1 - i) for i in range(sections)])
    with jax.named_scope("mirrorz"):
        both = lax.ppermute(far_b, ("section", "dp"),
                            [(s * shards + d, (sections - 1 - s) * shards + (d + ring) % shards) for s, d in devices])
    near_a, far_a = call(sum_a, (own_a, *got_a), (struct((share, wide), F32), quarter), [], "suma")
    with jax.named_scope("across"):
        far = lax.ppermute(far_a, "dp", [(d, (d + ring) % shards) for d in range(shards)])
    section_outputs = call(
        bind(forward_kernel, channels, side, True), (xa, xb, (new_inputs, 1), kernels, depth_bias, mixing),
        pair, fscratch, "fwd2")
    factor = float((2.0 * tick_count * shards * spots) ** (-0.5))
    grad_kernel, grad_bias, grad_mixing = call(
        bind(finish, channels, side, factor), (near_a, far, cross, both),
        (struct((side, side, 1, share), F32), struct((1, 1, share), F32), struct((share, 1, channels), F32)),
        [pltpu.VMEM((LANES, LANES), F32)], "finish")
    grad_kernel = jnp.transpose(grad_kernel[None], (0, 3, 1, 2, 4))
    grad_mixing = jnp.transpose(grad_mixing[None], (0, 2, 1, 3))
    return (section_outputs, input_grads, grad_kernel, grad_bias, grad_mixing)


def solution(mesh):
    return jax.shard_map(
        per_device,
        mesh=mesh,
        in_specs=(
            P(None, "section", "dp", None, None, None),
            P(None, None, "section", "dp", None, None, None),
            P(None, "section", "dp", None, None, None),
            P(None, None, "dp", None, None, None),
            P(None, None, "dp", None, None, None),
            P("section", None, None, None, None, None),
            P("section", None, None, None),
            P("section", None, None, None, None),
        ),
        out_specs=(
            P(None, "section", "dp", None, None, None),
            P(None, "section", "dp", None, None, None),
            P("section", None, None, None, "dp"),
            P("section", None, "dp"),
            P("section", None, "dp", None),
        ),
        check_vma=False,
    )
```
